512 devices in a mesh: row: 8 (over x_hi, y), pair: 64 (over z, x_lo, core).
Axes of the slice: x: 4 (x_hi: 2, x_lo: 2; x = x_hi * 2 + x_lo), y: 4, z: 16, core: 2. Of those that a mesh axis runs over, the one named last changes fastest.
Arguments:
- panel: float32 [16384, 16384], P('row', 'pair'), may hold values from -51 to 51
- slot_block: int32 [128], replicated, may hold values from 0 to 127, each once
Outputs:
- rotated: float32 [16384, 16384], P('row', 'pair')
The draws below stay inside these ranges and needn't reach their ends.
Inputs may be any that keep to these rules, and one draw needn't show every extreme that they name: `slot_block`: each block number appears once.
All inputs are finite; a program needn't handle non-finite values.
Results may differ from the reference program's by a relative error of at most 0.0003.
Values sent between devices are 32-bit elements; how exact they have to be, the bound alone decides.
No kernel may reach another device: no remote copies, remote signals or barrier semaphores. Data moves between devices by JAX's collectives and lax.ppermute only.
A program may use at most 64 MiB of HBM per device.

```python
import math
import jax
import jax.numpy as jnp
from jax import lax

B = 128
STEPS = 2
NS_ITERS = 3
PAIRS = 64
SLOTS = 128
NCOL = 16384
M = 16384


def draw_panel(key, part):
    keys = jax.random.split(jax.random.fold_in(key, 7), 3)
    base = jnp.clip(jax.random.normal(keys[0], (M, NCOL), jnp.float32), -6.0, 6.0)
    row_scale = jnp.exp(jax.random.uniform(keys[1], (M, 1), jnp.float32, math.log(0.3), math.log(3.0)))
    col_scale = jnp.exp(jax.random.uniform(keys[2], (1, NCOL), jnp.float32, math.log(0.5), math.log(2.0)))
    return base * row_scale * col_scale


def setup_inputs(seed: int = 0) -> dict:
    seeds = jax.random.split(jax.random.key(seed), 3)
    panel = draw_panel(jax.random.fold_in(seeds[2], 71), 0)
    slot_block = jax.random.permutation(seeds[1], SLOTS).astype(jnp.int32)
    return {"panel": panel, "slot_block": slot_block}


precise = lax.Precision.HIGHEST

def inverse_root(matrix):
    identity = jnp.eye(matrix.shape[0], dtype=matrix.dtype)
    approx = matrix
    root_inv = identity
    for sweep in range(NS_ITERS):
        factor = 1.5 * identity - 0.5 * jnp.dot(root_inv, approx, precision=precise)
        approx = jnp.dot(approx, factor, precision=precise)
        root_inv = jnp.dot(factor, root_inv, precision=precise)
    return root_inv / jnp.sqrt(5.0)

def couple(cross):
    identity = jnp.eye(cross.shape[0], dtype=cross.dtype)
    coupling = cross * (2.0 / jnp.sqrt(jnp.sum(cross * cross) + 1e-06))
    left = (identity + jnp.dot(coupling, coupling.T, precision=precise)) / 5.0
    right = (identity + jnp.dot(coupling.T, coupling, precision=precise)) / 5.0
    return (coupling, left, right)

def apply_rotation(first, second, coupling, left_inverse, right_inverse):
    new_first = jnp.dot(first + jnp.dot(second, coupling.T, precision=precise), left_inverse, precision=precise)
    new_second = jnp.dot(second - jnp.dot(first, coupling, precision=precise), right_inverse, precision=precise)
    return (new_first, new_second)

def move_slots(uppers, lowers):
    new_uppers = jnp.concatenate([uppers[0:1], lowers[0:1], uppers[1:-1]], axis=0)
    new_lowers = jnp.concatenate([lowers[1:], uppers[-1:]], axis=0)
    return (new_uppers, new_lowers)

def one_pair(items):
    upper, lower, upper_id, lower_id = items
    order_flag = upper_id < lower_id
    first = jnp.where(order_flag, upper, lower)
    second = jnp.where(order_flag, lower, upper)
    cross = jnp.dot(first.T, second, precision=precise)
    coupling, left, right = couple(cross)
    new_first, new_second = apply_rotation(first, second, coupling, inverse_root(left), inverse_root(right))
    return (jnp.where(order_flag, new_first, new_second), jnp.where(order_flag, new_second, new_first))

def reference(panel, slot_block):
    blocks = panel.reshape(M, PAIRS, 2, B)
    uppers = jnp.transpose(blocks[:, :, 0, :], (1, 0, 2))
    lowers = jnp.transpose(blocks[:, :, 1, :], (1, 0, 2))
    upper_ids = slot_block[:PAIRS]
    lower_ids = slot_block[PAIRS:]
    for step in range(STEPS):
        uppers, lowers = lax.map(one_pair, (uppers, lowers, upper_ids, lower_ids))
        uppers, lowers = move_slots(uppers, lowers)
        upper_ids, lower_ids = move_slots(upper_ids, lower_ids)
    stacked = jnp.stack([uppers, lowers], axis=1)
    return jnp.transpose(stacked, (2, 0, 1, 3)).reshape(M, NCOL)
```

```python
import jax
import jax.numpy as jnp
from jax import lax
from jax.experimental import pallas as pl
from jax.experimental.pallas import tpu as pltpu
from jax.sharding import PartitionSpec as P

NS_ITERS = 3
BLK = 128
CHUNK = 512


def halves(x):
    hi = x.astype(jnp.bfloat16)
    lo = (x - hi.astype(jnp.float32)).astype(jnp.bfloat16)
    return hi, lo


def mm_parts(a, b, dims):
    def dot(p, q):
        return lax.dot_general(p, q, (dims, ((), ())), preferred_element_type=jnp.float32)

    return dot(a[0], b[0]) + (dot(a[0], b[1]) + dot(a[1], b[0]))


def mm(a, b, dims=((1,), (0,))):
    return mm_parts(halves(a), halves(b), dims)


def eye():
    i = lax.broadcasted_iota(jnp.int32, (BLK, BLK), 0)
    j = lax.broadcasted_iota(jnp.int32, (BLK, BLK), 1)
    return jnp.where(i == j, 1.0, 0.0).astype(jnp.float32)


def inverse_roots(mats):
    ident = eye()
    ys = [halves(m) for m in mats]
    fs = [1.5 * ident - 0.5 * m for m in mats]
    zs = fs
    for sweep in range(1, NS_ITERS):
        fps = [halves(f) for f in fs]
        ys = [halves(mm_parts(y, f, ((1,), (0,)))) for y, f in zip(ys, fps)]
        zps = [halves(z) for z in zs]
        fs = [1.5 * ident - 0.5 * mm_parts(z, y, ((1,), (0,))) for z, y in zip(zps, ys)]
        zs = [mm_parts(halves(f), z, ((1,), (0,))) for f, z in zip(fs, zps)]
    return [z * (5.0**-0.5) for z in zs]


def tangent(cross, sign):
    return cross * (sign * 2.0 / jnp.sqrt(jnp.sum(cross * cross) + 1e-06))


def gram(x, y):
    xs = jnp.concatenate(halves(x), axis=1)
    ys = jnp.concatenate(halves(y), axis=1)
    return lax.dot_general(xs, ys, (((0,), (0,)), ((), ())), preferred_element_type=jnp.float32)


def gram_kernel(get, copies_ref, acc_ref):
    step = pl.program_id(0)

    @pl.when(step == 0)
    def _():
        acc_ref[...] = jnp.zeros_like(acc_ref)

    acc_ref[...] += gram(*get())

    @pl.when(step == pl.num_programs(0) - 1)
    def _():
        acc = acc_ref[...]
        total = (acc[:BLK, :BLK] + acc[BLK:, BLK:]) + (acc[:BLK, BLK:] + acc[BLK:, :BLK])
        for k in range(copies_ref.shape[0]):
            copies_ref[k] = total


def cross_of_panel(panel, count):
    rows, cols = panel.shape

    def kernel(x_ref, copies_ref, acc_ref):
        gram_kernel(lambda: (x_ref[:, :BLK], x_ref[:, BLK:]), copies_ref, acc_ref)

    return pl.pallas_call(
        kernel,
        grid=(rows // CHUNK,),
        in_specs=[pl.BlockSpec((CHUNK, cols), lambda i: (i, 0))],
        out_specs=pl.BlockSpec((count, BLK, BLK), lambda i: (0, 0, 0)),
        out_shape=jax.ShapeDtypeStruct((count, BLK, BLK), jnp.float32),
        scratch_shapes=[pltpu.VMEM((2 * BLK, 2 * BLK), jnp.float32)],
        name="cross_of_panel",
    )(panel)


def cross_of_blocks(x, y, count):
    rows = x.shape[0]

    def kernel(x_ref, y_ref, copies_ref, acc_ref):
        gram_kernel(lambda: (x_ref[...], y_ref[...]), copies_ref, acc_ref)

    return pl.pallas_call(
        kernel,
        grid=(rows // CHUNK,),
        in_specs=[pl.BlockSpec((CHUNK, BLK), lambda i: (i, 0))] * 2,
        out_specs=pl.BlockSpec((count, BLK, BLK), lambda i: (0, 0, 0)),
        out_shape=jax.ShapeDtypeStruct((count, BLK, BLK), jnp.float32),
        scratch_shapes=[pltpu.VMEM((2 * BLK, 2 * BLK), jnp.float32)],
        name="cross_of_blocks",
    )(x, y)


def rotate_panel(scalars, slot_block, gathered, panel):
    rows, cols = panel.shape
    count = gathered.shape[0]

    def kernel(pos_ref, ids_ref, g_ref, x_ref, one_ref, two_ref, whi_ref, wlo_ref):
        @pl.when(pl.program_id(0) == 0)
        def _():
            pos = pos_ref[0]
            pairs = pos_ref[1]
            sign = jnp.where(ids_ref[pos] < ids_ref[pairs + pos], 1.0, -1.0)
            upper_first = (lax.rem(pos, 2) == 1) | (pos == 0)
            cross = g_ref[0]
            for k in range(1, count):
                cross = cross + g_ref[k]
            kappa = tangent(cross, sign)
            kp = halves(kappa)
            ident = eye()
            left = (ident + mm_parts(kp, kp, ((1,), (1,)))) / 5.0
            right = (ident + mm_parts(kp, kp, ((0,), (0,)))) / 5.0
            linv, rinv = inverse_roots([left, right])
            lk = mm(kappa, linv, ((0,), (0,)))
            kr = mm(kappa, rinv)
            up = jnp.concatenate([linv, lk], axis=0)
            low = jnp.concatenate([-kr, rinv], axis=0)
            w = jnp.concatenate(
                [jnp.where(upper_first, up, low), jnp.where(upper_first, low, up)], axis=1
            )
            hi, lo = halves(w)
            whi_ref[...] = hi
            wlo_ref[...] = lo

        out = mm_parts(halves(x_ref[...]), (whi_ref[...], wlo_ref[...]), ((1,), (0,)))
        one_ref[...] = out[:, :BLK]
        two_ref[...] = out[:, BLK:]

    return pl.pallas_call(
        kernel,
        grid_spec=pltpu.PrefetchScalarGridSpec(
            num_scalar_prefetch=2,
            grid=(rows // CHUNK,),
            in_specs=[
                pl.BlockSpec((count, BLK, BLK), lambda i, *_: (0, 0, 0)),
                pl.BlockSpec((CHUNK, cols), lambda i, *_: (i, 0)),
            ],
            out_specs=[pl.BlockSpec((CHUNK, BLK), lambda i, *_: (i, 0))] * 2,
            scratch_shapes=[pltpu.VMEM((2 * BLK, 2 * BLK), jnp.bfloat16)] * 2,
        ),
        out_shape=[jax.ShapeDtypeStruct((rows, BLK), jnp.float32)] * 2,
        name="rotate_panel",
    )(scalars, slot_block, gathered, panel)


def received_coefficients(cross, sign, swap):
    kappa = tangent(jnp.where(swap, cross.T, cross), jnp.where(swap, -sign, sign))
    kp = halves(kappa)
    right = (eye() + mm_parts(kp, kp, ((0,), (0,)))) / 5.0
    (rinv,) = inverse_roots([right])
    other = -mm(kappa, rinv)
    return jnp.where(swap, rinv, other), jnp.where(swap, other, rinv)


def rotate_received(scalars, slot_block, cross, local, received, primary, out):
    rows = local.shape[0]

    def kernel(pos_ref, ids_ref, m_ref, x_ref, y_ref, *rest):
        o_ref, whi_ref, wlo_ref = rest[-3:]

        @pl.when(pl.program_id(0) == 0)
        def _():
            pos = pos_ref[0]
            pairs = pos_ref[1]
            odd = lax.rem(pos, 2) == 1
            upper_first = odd | (pos == 0)
            if primary:
                mine = jnp.where(upper_first, pairs + pos, pos)
                theirs = jnp.where(
                    odd,
                    jnp.where(pos == 1, 0, pos - 2),
                    jnp.where(pos == pairs - 2, pairs - 1, pairs + pos + 2),
                )
                swap = pos == 1
                cross = m_ref[...]
            else:
                mine = jnp.where(upper_first, pos, pairs + pos)
                theirs = jnp.where(
                    odd,
                    jnp.where(pos == pairs - 1, pairs - 2, pairs + pos + 2),
                    jnp.where(pos == 0, pairs + 1, jnp.where(pos == 2, pairs, pos - 2)),
                )
                swap = pos == 0
                cross = m_ref[...].T
            sign = jnp.where(ids_ref[mine] < ids_ref[theirs], 1.0, -1.0)
            cx, cy = received_coefficients(cross, sign, swap)
            hi, lo = halves(jnp.concatenate([cx, cy], axis=0))
            whi_ref[...] = hi
            wlo_ref[...] = lo

        z = jnp.concatenate([x_ref[...], y_ref[...]], axis=1)
        o_ref[...] = mm_parts(halves(z), (whi_ref[...], wlo_ref[...]), ((1,), (0,)))

    block = pl.BlockSpec((CHUNK, BLK), lambda i, *_: (i, 0))
    half = 3 if primary else 2
    operands = [scalars, slot_block, cross, local, received]
    in_specs = [pl.BlockSpec((BLK, BLK), lambda i, *_: (0, 0)), block, block]
    aliases = {}
    if out is not None:
        operands.append(out)
        in_specs.append(pl.BlockSpec(memory_space=pl.ANY))
        aliases = {5: 0}
    return pl.pallas_call(
        kernel,
        grid_spec=pltpu.PrefetchScalarGridSpec(
            num_scalar_prefetch=2,
            grid=(rows // CHUNK,),
            in_specs=in_specs,
            out_specs=pl.BlockSpec((CHUNK, BLK), lambda i, s, *_: (i, s[half])),
            scratch_shapes=[pltpu.VMEM((2 * BLK, BLK), jnp.bfloat16)] * 2,
        ),
        out_shape=jax.ShapeDtypeStruct((rows, 2 * BLK), jnp.float32),
        input_output_aliases=aliases,
        name="rotate_primary" if primary else "rotate_secondary",
    )(*operands)


def exchange(copies):
    return lax.all_to_all(copies, "row", split_axis=0, concat_axis=0, tiled=True)


def per_device(panel, slot_block):
    count = lax.axis_size("row")
    pairs = lax.axis_size("pair")
    position = lax.axis_index("pair")
    odd = lax.rem(position, 2)
    scalars = jnp.stack([position, jnp.full_like(position, pairs), odd, 1 - odd]).astype(jnp.int32)
    there = [(q, q + 2) for q in range(1, pairs - 2, 2)] + [(q, q - 2) for q in range(2, pairs, 2)]
    there += [(0, 1), (pairs - 1, pairs - 2)]
    back = [(target, source) for source, target in there]

    one, two = rotate_panel(scalars, slot_block, exchange(cross_of_panel(panel, count)), panel)
    first = lax.ppermute(one, "pair", there)
    first, two = lax.optimization_barrier((first, two))
    second = lax.ppermute(two, "pair", back)
    cross = jnp.sum(exchange(cross_of_blocks(two, first, count)), axis=0)
    cross_back = lax.ppermute(cross, "pair", back)
    out = rotate_received(scalars, slot_block, cross, two, first, True, None)
    return rotate_received(scalars, slot_block, cross_back, one, second, False, out)


def solution(mesh):
    return jax.shard_map(
        per_device,
        mesh=mesh,
        in_specs=(P("row", "pair"), P()),
        out_specs=P("row", "pair"),
        check_vma=False,
    )
```

```python
import functools

import jax
import jax.numpy as jnp
from jax import lax
from jax.experimental import pallas as pl
from jax.experimental.pallas import tpu as pltpu
from jax.sharding import PartitionSpec as P

NS_ITERS = 3
BLK = 128
CHUNK = 256
TAIL = 256
VMEM = pl.BlockSpec(memory_space=pltpu.VMEM)
SMEM = pl.BlockSpec(memory_space=pltpu.SMEM)
ANY = pl.BlockSpec(memory_space=pl.ANY)
NN = ((1,), (0,))
TN = ((0,), (0,))
NT = ((1,), (1,))


def call(kernel, out_shape, in_specs, out_specs, flops, scratch=(), aliases=None):
    return pl.pallas_call(
        kernel,
        out_shape=out_shape,
        in_specs=in_specs,
        out_specs=out_specs,
        scratch_shapes=list(scratch),
        input_output_aliases=aliases or {},
        compiler_params=pltpu.CompilerParams(vmem_limit_bytes=16 << 20),
        cost_estimate=pl.CostEstimate(flops=flops, bytes_accessed=2 << 20, transcendentals=0),
    )


def halves(x):
    hi = x.astype(jnp.bfloat16)
    lo = (x - hi.astype(jnp.float32)).astype(jnp.bfloat16)
    return hi, lo


def mm_parts(a, b, dims=NN):
    def dot(p, q):
        return lax.dot_general(p, q, (dims, ((), ())), preferred_element_type=jnp.float32)

    return dot(a[0], b[0]) + (dot(a[0], b[1]) + dot(a[1], b[0]))


def mm(a, b, dims=NN):
    return mm_parts(halves(a), halves(b), dims)


def eye():
    i = lax.broadcasted_iota(jnp.int32, (BLK, BLK), 0)
    j = lax.broadcasted_iota(jnp.int32, (BLK, BLK), 1)
    return jnp.where(i == j, 1.0, 0.0).astype(jnp.float32)


def inverse_roots(mats):
    ident = eye()
    ys = [halves(m) for m in mats]
    fs = [1.5 * ident - 0.5 * m for m in mats]
    zs = fs
    for _ in range(1, NS_ITERS):
        fps = [halves(f) for f in fs]
        ys = [halves(mm_parts(y, f)) for y, f in zip(ys, fps)]
        zps = [halves(z) for z in zs]
        fs = [1.5 * ident - 0.5 * mm_parts(z, y) for z, y in zip(zps, ys)]
        zs = [mm_parts(halves(f), z) for f, z in zip(fs, zps)]
    return [z * (5.0**-0.5) for z in zs]


def tangent(cross, sign):
    return cross * (sign * 2.0 / jnp.sqrt(jnp.sum(cross * cross) + 1e-06))


def gram(pairs):
    acc = None
    for x, y in pairs:
        xs = jnp.concatenate(halves(x), axis=1)
        ys = jnp.concatenate(halves(y), axis=1)
        part = lax.dot_general(xs, ys, (TN, ((), ())), preferred_element_type=jnp.float32)
        acc = part if acc is None else acc + part
    return acc


def fold(acc):
    return (acc[:BLK, :BLK] + acc[BLK:, BLK:]) + (acc[:BLK, BLK:] + acc[BLK:, :BLK])


def chunks(rows):
    return [pl.ds(r, min(CHUNK, rows - r)) for r in range(0, rows, CHUNK)]


def cross_of_panel(panel, count):
    rows = panel.shape[0]

    def kernel(x_ref, copies_ref):
        total = fold(gram((x_ref[c, :BLK], x_ref[c, BLK:]) for c in chunks(rows)))
        for k in range(count):
            copies_ref[k] = total

    shape = jax.ShapeDtypeStruct((count, BLK, BLK), jnp.float32)
    return call(kernel, shape, [VMEM], VMEM, rows * BLK * BLK * 8)(panel)


def cross_head(local, received):
    rows = received.shape[0]

    def kernel(x_ref, y_ref, acc_ref):
        acc_ref[...] = gram((x_ref[c, :], y_ref[c, :]) for c in chunks(rows))

    shape = jax.ShapeDtypeStruct((2 * BLK, 2 * BLK), jnp.float32)
    return call(kernel, shape, [VMEM] * 2, VMEM, rows * BLK * BLK * 8)(local, received)


def cross_tail(acc, local, received, count):
    rows = received.shape[0]
    base = local.shape[0] - rows

    def kernel(acc_ref, x_ref, y_ref, copies_ref):
        x_tail = x_ref.at[base:, :]
        total = fold(acc_ref[...] + gram((x_tail[c, :], y_ref[c, :]) for c in chunks(rows)))
        for k in range(count):
            copies_ref[k] = total

    shape = jax.ShapeDtypeStruct((count, BLK, BLK), jnp.float32)
    return call(kernel, shape, [VMEM] * 3, VMEM, rows * BLK * BLK * 8)(acc, local, received)


def total_of(parts):
    def kernel(p_ref, o_ref):
        total = p_ref[0]
        for k in range(1, parts.shape[0]):
            total = total + p_ref[k]
        o_ref[...] = total

    shape = jax.ShapeDtypeStruct(parts.shape[1:], parts.dtype)
    return call(kernel, shape, [VMEM], VMEM, parts.size)(parts)


def rotate_panel(slot_block, gathered, panel, pairs):
    rows = panel.shape[0]
    count = gathered.shape[0]
    head = rows - TAIL

    def kernel(ids_ref, g_ref, x_ref, head_ref, tail_ref, two_ref):
        pos = lax.axis_index("pair")
        sign = jnp.where(ids_ref[pos] < ids_ref[pairs + pos], 1.0, -1.0)
        upper_first = (lax.rem(pos, 2) == 1) | (pos == 0)
        cross = g_ref[0]
        for k in range(1, count):
            cross = cross + g_ref[k]
        kappa = tangent(cross, sign)
        kp = halves(kappa)
        ident = eye()
        left = (ident + mm_parts(kp, kp, NT)) / 5.0
        right = (ident + mm_parts(kp, kp, TN)) / 5.0
        linv, rinv = inverse_roots([left, right])
        up = jnp.concatenate([linv, mm(kappa, linv, TN)], axis=0)
        low = jnp.concatenate([-mm(kappa, rinv), rinv], axis=0)
        w = jnp.concatenate(
            [jnp.where(upper_first, up, low), jnp.where(upper_first, low, up)], axis=1
        )
        wp = halves(w)
        for c in chunks(rows):
            out = mm_parts(halves(x_ref[c, :]), wp)
            if c.start < head:
                head_ref[c, :] = out[:, :BLK]
            else:
                tail_ref[pl.ds(c.start - head, c.size), :] = out[:, :BLK]
            two_ref[c, :] = out[:, BLK:]

    shapes = [jax.ShapeDtypeStruct((n, BLK), jnp.float32) for n in (head, TAIL, rows)]
    return call(
        kernel, shapes, [SMEM, VMEM, VMEM], [VMEM] * 3, rows * BLK * BLK * 24
    )(slot_block, gathered, panel)


def rotate_received(slot_block, crosses, locals_, received, out, pairs, primary):
    rows = sum(x.shape[0] for x in received)
    n_loc, n_rec = len(locals_), len(received)

    def rows_of(refs, c):
        start = c.start
        for ref in refs:
            if start < ref.shape[0]:
                return ref[pl.ds(start, c.size), :]
            start -= ref.shape[0]

    def kernel(*refs):
        ids_ref, m_ref, n_ref = refs[:3]
        x_refs = refs[3 : 3 + n_loc]
        y_refs = refs[3 + n_loc : 3 + n_loc + n_rec]
        o_ref, buf_ref, sems = refs[-3:]
        pos = lax.axis_index("pair")
        odd = lax.rem(pos, 2) == 1
        upper_first = odd | (pos == 0)
        if primary:
            mine = jnp.where(upper_first, pairs + pos, pos)
            theirs = jnp.where(
                odd,
                jnp.where(pos == 1, 0, pos - 2),
                jnp.where(pos == pairs - 2, pairs - 1, pairs + pos + 2),
            )
            swap = pos == 1
            column = jnp.where(odd, 0, BLK)
            cross = m_ref[...] + n_ref[...]
        else:
            mine = jnp.where(upper_first, pos, pairs + pos)
            theirs = jnp.where(
                odd,
                jnp.where(pos == pairs - 1, pairs - 2, pairs + pos + 2),
                jnp.where(pos == 0, pairs + 1, jnp.where(pos == 2, pairs, pos - 2)),
            )
            swap = pos == 0
            column = jnp.where(odd, BLK, 0)
            cross = (m_ref[...] + n_ref[...]).T
        sign = jnp.where(ids_ref[mine] < ids_ref[theirs], 1.0, -1.0)
        kappa = tangent(jnp.where(swap, cross.T, cross), jnp.where(swap, -sign, sign))
        kp = halves(kappa)
        (rinv,) = inverse_roots([(eye() + mm_parts(kp, kp, TN)) / 5.0])
        other = -mm(kappa, rinv)
        w = jnp.concatenate(
            [jnp.where(swap, rinv, other), jnp.where(swap, other, rinv)], axis=0
        )
        wp = halves(w)
        column = pl.multiple_of(column, BLK)
        copies = []
        for i, c in enumerate(chunks(rows)):
            z = jnp.concatenate([rows_of(x_refs, c), rows_of(y_refs, c)], axis=1)
            buf_ref[c, :] = mm_parts(halves(z), wp)
            copy = pltpu.make_async_copy(
                buf_ref.at[c, :], o_ref.at[c, pl.ds(column, BLK)], sems.at[i]
            )
            copy.start()
            copies.append(copy)
        for copy in copies:
            copy.wait()

    operands = [slot_block, *crosses, *locals_, *received]
    in_specs = [SMEM] + [VMEM] * (len(operands) - 1)
    aliases = {}
    if out is not None:
        aliases = {len(operands): 0}
        operands.append(out)
        in_specs.append(ANY)
    return call(
        kernel,
        jax.ShapeDtypeStruct((rows, 2 * BLK), jnp.float32),
        in_specs,
        ANY,
        rows * BLK * BLK * 12,
        scratch=[
            pltpu.VMEM((rows, BLK), jnp.float32),
            pltpu.SemaphoreType.DMA((rows // CHUNK,)),
        ],
        aliases=aliases,
    )(*operands)


def per_device(panel, slot_block):
    count = lax.axis_size("row")
    pairs = lax.axis_size("pair")
    half = count // 2
    there = [(q, q + 2) for q in range(1, pairs - 2, 2)] + [(q, q - 2) for q in range(2, pairs, 2)]
    there += [(0, 1), (pairs - 1, pairs - 2)]
    back = [(target, source) for source, target in there]
    across = [(r, (r + half) % count) for r in range(count)]
    back_across = [
        (r * pairs + source, s * pairs + target) for r, s in across for source, target in back
    ]
    near = [list(range(half)), list(range(half, count))]
    exchange = functools.partial(
        lax.all_to_all, axis_name="row", split_axis=0, concat_axis=0, tiled=True
    )

    gathered = exchange(cross_of_panel(panel, count))
    one_head, one_tail, two = rotate_panel(slot_block, gathered, panel, pairs)
    got_head = lax.ppermute(one_head, "pair", there)
    got_tail = lax.ppermute(one_tail, "pair", there)
    got_head, two = lax.optimization_barrier((got_head, two))
    second = lax.ppermute(two, "pair", back)
    acc = cross_head(two, got_head)
    part = total_of(
        exchange(cross_tail(acc, two, got_tail, half), axis_index_groups=near)
    )
    other = lax.ppermute(part, "row", across)
    back_near = lax.ppermute(part, "pair", back)
    back_far = lax.ppermute(part, ("row", "pair"), back_across)
    out = rotate_received(slot_block, [part, other], [two], [got_head, got_tail], None, pairs, True)
    return rotate_received(
        slot_block,
        [back_near, back_far],
        [one_head, one_tail],
        [second],
        out,
        pairs,
        False,
    )


def solution(mesh):
    return jax.shard_map(
        per_device,
        mesh=mesh,
        in_specs=(P("row", "pair"), P()),
        out_specs=P("row", "pair"),
        check_vma=False,
    )
```

```python
import functools

import jax
import jax.numpy as jnp
from jax import lax
from jax.experimental import pallas as pl
from jax.experimental.pallas import tpu as pltpu
from jax.sharding import PartitionSpec as P

NS_ITERS = 3
BLK = 128
CHUNK = 256
SPIN = 1500
VMEM = pl.BlockSpec(memory_space=pltpu.VMEM)
SMEM = pl.BlockSpec(memory_space=pltpu.SMEM)
ANY = pl.BlockSpec(memory_space=pl.ANY)
NN = ((1,), (0,))
TN = ((0,), (0,))
NT = ((1,), (1,))


def call(kernel, out_shape, in_specs, out_specs, flops, scratch=(), aliases=None):
    return pl.pallas_call(
        kernel,
        out_shape=out_shape,
        in_specs=in_specs,
        out_specs=out_specs,
        scratch_shapes=list(scratch),
        input_output_aliases=aliases or {},
        compiler_params=pltpu.CompilerParams(vmem_limit_bytes=16 << 20),
        cost_estimate=pl.CostEstimate(flops=flops, bytes_accessed=2 << 20, transcendentals=0),
    )


def halves(x):
    hi = x.astype(jnp.bfloat16)
    lo = (x - hi.astype(jnp.float32)).astype(jnp.bfloat16)
    return hi, lo


def mm_parts(a, b, dims=NN):
    def dot(p, q):
        return lax.dot_general(p, q, (dims, ((), ())), preferred_element_type=jnp.float32)

    return dot(a[0], b[0]) + (dot(a[0], b[1]) + dot(a[1], b[0]))


def dot(a, b, dims=NN):
    return lax.dot_general(a, b, (dims, ((), ())), preferred_element_type=jnp.float32)


def mm_narrow(a, b):
    ah, al = halves(a)
    wide = dot(ah, jnp.concatenate(b, axis=1))
    return (wide[:, :BLK] + wide[:, BLK:]) + dot(al, b[0])


def mm(a, b, dims=NN):
    return mm_parts(halves(a), halves(b), dims)


def eye():
    i = lax.broadcasted_iota(jnp.int32, (BLK, BLK), 0)
    j = lax.broadcasted_iota(jnp.int32, (BLK, BLK), 1)
    return jnp.where(i == j, 1.0, 0.0).astype(jnp.float32)


def inverse_roots(mats):
    ident = eye()
    ys = [halves(m) for m in mats]
    fs = [1.5 * ident - 0.5 * m for m in mats]
    zs = fs
    for _ in range(1, NS_ITERS):
        fps = [halves(f) for f in fs]
        ys = [halves(mm_parts(y, f)) for y, f in zip(ys, fps)]
        zps = [halves(z) for z in zs]
        fs = [1.5 * ident - 0.5 * mm_parts(z, y) for z, y in zip(zps, ys)]
        zs = [mm_parts(halves(f), z) for f, z in zip(fs, zps)]
    return [z * (5.0**-0.5) for z in zs]


def tangent(cross, sign):
    return cross * (sign * 2.0 / jnp.sqrt(jnp.sum(cross * cross) + 1e-06))


def gram(pairs):
    acc = None
    for x, y in pairs:
        xs = jnp.concatenate(halves(x), axis=1)
        ys = jnp.concatenate(halves(y), axis=1)
        part = lax.dot_general(xs, ys, (TN, ((), ())), preferred_element_type=jnp.float32)
        acc = part if acc is None else acc + part
    return acc


def fold(acc):
    return (acc[:BLK, :BLK] + acc[BLK:, BLK:]) + (acc[:BLK, BLK:] + acc[BLK:, :BLK])


def chunks(rows):
    return [pl.ds(r, min(CHUNK, rows - r)) for r in range(0, rows, CHUNK)]


def cross_of_panel(panel, count):
    rows = panel.shape[0]

    def kernel(x_ref, copies_ref):
        total = fold(gram((x_ref[c, :BLK], x_ref[c, BLK:]) for c in chunks(rows)))
        for k in range(count):
            copies_ref[k] = total

    shape = jax.ShapeDtypeStruct((count, BLK, BLK), jnp.float32)
    return call(kernel, shape, [VMEM], VMEM, rows * BLK * BLK * 8)(panel)


def cross_of_blocks(local, received, count):
    rows = received.shape[0]

    def kernel(x_ref, y_ref, copies_ref):
        total = fold(gram((x_ref[c, :], y_ref[c, :]) for c in chunks(rows)))
        for k in range(count):
            copies_ref[k] = total

    shape = jax.ShapeDtypeStruct((count, BLK, BLK), jnp.float32)
    return call(kernel, shape, [VMEM] * 2, VMEM, rows * BLK * BLK * 8)(local, received)


def hold_ends(got, block, pairs):
    def kernel(g_ref, x_ref, o_ref, s_ref):
        pos = lax.axis_index("pair")
        at_end = (pos == 0) | (pos == pairs - 1)

        @pl.when(at_end)
        def _():
            s_ref[...] = lax.fori_loop(0, SPIN, lambda i, x: x * 0.5 + 1.0, g_ref[0:8, :])

    shapes = [
        jax.ShapeDtypeStruct(block.shape, block.dtype),
        jax.ShapeDtypeStruct((8, BLK), block.dtype),
    ]
    return call(kernel, shapes, [VMEM, ANY], [ANY, VMEM], 1000, aliases={1: 0})(got, block)[0]


def total_of(parts, copies):
    def kernel(*refs):
        total = None
        for ref in refs[:-1]:
            for k in range(ref.shape[0]):
                total = ref[k] if total is None else total + ref[k]
        for k in range(copies):
            refs[-1][k] = total

    shape = jax.ShapeDtypeStruct((copies, BLK, BLK), jnp.float32)
    return call(kernel, shape, [VMEM] * len(parts), VMEM, BLK * BLK * 4)(*parts)


def rotate_panel(slot_block, gathered, panel, pairs):
    rows = panel.shape[0]
    count = gathered.shape[0]

    def kernel(ids_ref, g_ref, x_ref, one_ref, two_ref):
        pos = lax.axis_index("pair")
        sign = jnp.where(ids_ref[pos] < ids_ref[pairs + pos], 1.0, -1.0)
        upper_first = (lax.rem(pos, 2) == 1) | (pos == 0)
        cross = g_ref[0]
        for k in range(1, count):
            cross = cross + g_ref[k]
        kappa = tangent(cross, sign)
        kp = halves(kappa)
        ident = eye()
        left = (ident + mm_parts(kp, kp, NT)) / 5.0
        right = (ident + mm_parts(kp, kp, TN)) / 5.0
        linv, rinv = inverse_roots([left, right])
        up = jnp.concatenate([linv, mm(kappa, linv, TN)], axis=0)
        low = jnp.concatenate([-mm(kappa, rinv), rinv], axis=0)
        w = jnp.concatenate(
            [jnp.where(upper_first, up, low), jnp.where(upper_first, low, up)], axis=1
        )
        wp = halves(w)
        for c in chunks(rows):
            out = mm_parts(halves(x_ref[c, :]), wp)
            one_ref[c, :] = out[:, :BLK]
            two_ref[c, :] = out[:, BLK:]

    shapes = [jax.ShapeDtypeStruct((n, BLK), jnp.float32) for n in (rows, rows)]
    return call(
        kernel, shapes, [SMEM, VMEM, VMEM], [VMEM] * 2, rows * BLK * BLK * 24
    )(slot_block, gathered, panel)


def rotate_pairs(slot_block, crosses, locals_, received, pairs):
    rows = locals_[0].shape[0]
    steps = rows // CHUNK

    def kernel(ids_ref, a_ref, b_ref, c_ref, d_ref, x1_ref, y1_ref, x2_ref, y2_ref, *rest):
        o_ref, buf_ref, sems = rest
        pos = lax.axis_index("pair")
        odd = lax.rem(pos, 2) == 1
        upper_first = odd | (pos == 0)
        mine = [jnp.where(upper_first, pairs + pos, pos), jnp.where(upper_first, pos, pairs + pos)]
        theirs = [
            jnp.where(
                odd,
                jnp.where(pos == 1, 0, pos - 2),
                jnp.where(pos == pairs - 2, pairs - 1, pairs + pos + 2),
            ),
            jnp.where(
                odd,
                jnp.where(pos == pairs - 1, pairs - 2, pairs + pos + 2),
                jnp.where(pos == 0, pairs + 1, jnp.where(pos == 2, pairs, pos - 2)),
            ),
        ]
        swaps = [pos == 1, pos == 0]
        crosses = [a_ref[0] + b_ref[0], c_ref[0] + d_ref[0]]
        kappas = []
        for k in range(2):
            flip = swaps[k] if k == 0 else jnp.logical_not(swaps[k])
            sign = jnp.where(ids_ref[mine[k]] < ids_ref[theirs[k]], 1.0, -1.0)
            cross = jnp.where(flip, crosses[k].T, crosses[k])
            kappas.append(tangent(cross, jnp.where(swaps[k], -sign, sign)))
        ident = eye()
        rights = []
        for kappa in kappas:
            kp = halves(kappa)
            rights.append((ident + mm_parts(kp, kp, TN)) / 5.0)
        rinvs = inverse_roots(rights)
        wps = []
        for k in range(2):
            other = -mm(kappas[k], rinvs[k])
            w = [jnp.where(swaps[k], rinvs[k], other), jnp.where(swaps[k], other, rinvs[k])]
            wps.append(halves(jnp.concatenate(w, axis=0)))
        columns = [jnp.where(odd, 0, BLK), jnp.where(odd, BLK, 0)]
        copies = []
        for i, c in enumerate(chunks(rows)):
            for k, (x_ref, y_ref) in enumerate(((x1_ref, y1_ref), (x2_ref, y2_ref))):
                z = jnp.concatenate([x_ref[c, :], y_ref[c, :]], axis=1)
                buf_ref[k, c, :] = mm_narrow(z, wps[k])
                column = pl.multiple_of(columns[k], BLK)
                copy = pltpu.make_async_copy(
                    buf_ref.at[k, c, :], o_ref.at[c, pl.ds(column, BLK)], sems.at[k, i]
                )
                copy.start()
                copies.append(copy)
        for copy in copies:
            copy.wait()

    operands = [slot_block, *crosses, locals_[0], received[0], locals_[1], received[1]]
    return call(
        kernel,
        jax.ShapeDtypeStruct((rows, 2 * BLK), jnp.float32),
        [SMEM] + [VMEM] * 8,
        ANY,
        rows * BLK * BLK * 24,
        scratch=[
            pltpu.VMEM((2, rows, BLK), jnp.float32),
            pltpu.SemaphoreType.DMA((2, steps)),
        ],
    )(*operands)


def per_device(panel, slot_block):
    count = lax.axis_size("row")
    pairs = lax.axis_size("pair")
    half = count // 2
    there = [(q, q + 2) for q in range(1, pairs - 2, 2)] + [(q, q - 2) for q in range(2, pairs, 2)]
    there += [(0, 1), (pairs - 1, pairs - 2)]
    back = [(target, source) for source, target in there]
    across = [(r, (r + half) % count) for r in range(count)]
    back_across = [
        (r * pairs + source, s * pairs + target) for r, s in across for source, target in back
    ]
    near = [list(range(half)), list(range(half, count))]
    exchange = functools.partial(
        lax.all_to_all, axis_name="row", split_axis=0, concat_axis=0, tiled=True
    )

    gathered = exchange(cross_of_panel(panel, count))
    one, two = rotate_panel(slot_block, gathered, panel, pairs)
    first = lax.ppermute(one, "pair", there)
    two = hold_ends(first, two, pairs)
    second = lax.ppermute(two, "pair", back)
    partial = cross_of_blocks(two, first, half)
    part = total_of([exchange(partial, axis_index_groups=near)], 1)
    back_near = lax.ppermute(part, "pair", back)
    back_far = lax.ppermute(part, ("row", "pair"), back_across)
    other = lax.ppermute(part, "row", across)
    return rotate_pairs(
        slot_block, [part, other, back_near, back_far], [two, one], [first, second], pairs
    )


def solution(mesh):
    return jax.shard_map(
        per_device,
        mesh=mesh,
        in_specs=(P("row", "pair"), P()),
        out_specs=P("row", "pair"),
        check_vma=False,
    )
```

```python
import functools

import jax
import jax.numpy as jnp
from jax import lax
from jax.experimental import pallas as pl
from jax.experimental.pallas import tpu as pltpu
from jax.sharding import PartitionSpec as P

NS_ITERS = 3
BLK = 128
CHUNK = 256
SPIN = 1500
VMEM = pl.BlockSpec(memory_space=pltpu.VMEM)
SMEM = pl.BlockSpec(memory_space=pltpu.SMEM)
ANY = pl.BlockSpec(memory_space=pl.ANY)
NN = ((1,), (0,))
TN = ((0,), (0,))
NT = ((1,), (1,))


def call(kernel, out_shape, in_specs, out_specs, flops, scratch=(), aliases=None):
    return pl.pallas_call(
        kernel,
        out_shape=out_shape,
        in_specs=in_specs,
        out_specs=out_specs,
        scratch_shapes=list(scratch),
        input_output_aliases=aliases or {},
        compiler_params=pltpu.CompilerParams(vmem_limit_bytes=16 << 20),
        cost_estimate=pl.CostEstimate(flops=flops, bytes_accessed=2 << 20, transcendentals=0),
    )


def halves(x):
    hi = x.astype(jnp.bfloat16)
    lo = (x - hi.astype(jnp.float32)).astype(jnp.bfloat16)
    return hi, lo


def mm_parts(a, b, dims=NN):
    def dot(p, q):
        return lax.dot_general(p, q, (dims, ((), ())), preferred_element_type=jnp.float32)

    return dot(a[0], b[0]) + (dot(a[0], b[1]) + dot(a[1], b[0]))


def dot(a, b, dims=NN):
    return lax.dot_general(a, b, (dims, ((), ())), preferred_element_type=jnp.float32)


def mm_narrow(a, b):
    ah, al = halves(a)
    wide = dot(ah, jnp.concatenate(b, axis=1))
    return (wide[:, :BLK] + wide[:, BLK:]) + dot(al, b[0])


def mm(a, b, dims=NN):
    return mm_parts(halves(a), halves(b), dims)


def eye():
    i = lax.broadcasted_iota(jnp.int32, (BLK, BLK), 0)
    j = lax.broadcasted_iota(jnp.int32, (BLK, BLK), 1)
    return jnp.where(i == j, 1.0, 0.0).astype(jnp.float32)


def inverse_roots(mats):
    ident = eye()
    ys = [halves(m) for m in mats]
    fs = [1.5 * ident - 0.5 * m for m in mats]
    zs = fs
    for _ in range(1, NS_ITERS):
        fps = [halves(f) for f in fs]
        ys = [halves(mm_parts(y, f)) for y, f in zip(ys, fps)]
        zps = [halves(z) for z in zs]
        fs = [1.5 * ident - 0.5 * mm_parts(z, y) for z, y in zip(zps, ys)]
        zs = [mm_parts(halves(f), z) for f, z in zip(fs, zps)]
    return [z * (5.0**-0.5) for z in zs]


def tangent(cross, sign):
    return cross * (sign * 2.0 / jnp.sqrt(jnp.sum(cross * cross) + 1e-06))


def gram(pairs):
    acc = None
    for x, y in pairs:
        xs = jnp.concatenate(halves(x), axis=1)
        ys = jnp.concatenate(halves(y), axis=1)
        part = lax.dot_general(xs, ys, (TN, ((), ())), preferred_element_type=jnp.float32)
        acc = part if acc is None else acc + part
    return acc


def fold(acc):
    return (acc[:BLK, :BLK] + acc[BLK:, BLK:]) + (acc[:BLK, BLK:] + acc[BLK:, :BLK])


def chunks(rows):
    return [pl.ds(r, min(CHUNK, rows - r)) for r in range(0, rows, CHUNK)]


def cross_of_panel(panel, count):
    rows = panel.shape[0]

    def kernel(x_ref, copies_ref):
        total = fold(gram((x_ref[c, :BLK], x_ref[c, BLK:]) for c in chunks(rows)))
        for k in range(count):
            copies_ref[k] = total

    shape = jax.ShapeDtypeStruct((count, BLK, BLK), jnp.float32)
    return call(kernel, shape, [VMEM], VMEM, rows * BLK * BLK * 8)(panel)


def cross_of_blocks(local, received, count, pairs):
    rows = received.shape[0]

    def kernel(x_ref, y_ref, copies_ref, o_ref):
        total = fold(gram((x_ref[c, :], y_ref[c, :]) for c in chunks(rows)))
        for k in range(count):
            copies_ref[k] = total
        pos = lax.axis_index("pair")

        @pl.when((pos == 1) | (pos == pairs - 2))
        def _():
            start = jnp.full((8, BLK), pos, jnp.float32)
            turned = lax.fori_loop(0, SPIN, lambda i, x: x * 0.5 + 1.0, start)
            copies_ref[0, 0:8, :] = jnp.where(turned > 1000.0, turned, total[0:8, :])

    shapes = [
        jax.ShapeDtypeStruct((count, BLK, BLK), jnp.float32),
        jax.ShapeDtypeStruct(local.shape, local.dtype),
    ]
    return call(
        kernel, shapes, [VMEM] * 2, [VMEM, ANY], rows * BLK * BLK * 8, aliases={0: 1}
    )(local, received)


def total_of(parts, copies):
    def kernel(*refs):
        total = None
        for ref in refs[:-1]:
            for k in range(ref.shape[0]):
                total = ref[k] if total is None else total + ref[k]
        for k in range(copies):
            refs[-1][k] = total

    shape = jax.ShapeDtypeStruct((copies, BLK, BLK), jnp.float32)
    return call(kernel, shape, [VMEM] * len(parts), VMEM, BLK * BLK * 4)(*parts)


def rotate_first(slot_block, gathered, panel, pairs):
    rows = panel.shape[0]
    count = gathered.shape[0]

    def kernel(ids_ref, g_ref, x_ref, two_ref, w_ref):
        pos = lax.axis_index("pair")
        sign = jnp.where(ids_ref[pos] < ids_ref[pairs + pos], 1.0, -1.0)
        upper_first = (lax.rem(pos, 2) == 1) | (pos == 0)
        cross = g_ref[0]
        for k in range(1, count):
            cross = cross + g_ref[k]
        kappa = tangent(cross, sign)
        kp = halves(kappa)
        ident = eye()
        left = (ident + mm_parts(kp, kp, NT)) / 5.0
        right = (ident + mm_parts(kp, kp, TN)) / 5.0
        linv, rinv = inverse_roots([left, right])
        up = jnp.concatenate([linv, mm(kappa, linv, TN)], axis=0)
        low = jnp.concatenate([-mm(kappa, rinv), rinv], axis=0)
        w_ref[...] = jnp.where(upper_first, up, low)
        wp = halves(jnp.where(upper_first, low, up))
        for c in chunks(rows):
            two_ref[c, :] = mm_narrow(x_ref[c, :], wp)

    shapes = [
        jax.ShapeDtypeStruct((rows, BLK), jnp.float32),
        jax.ShapeDtypeStruct((2 * BLK, BLK), jnp.float32),
    ]
    return call(
        kernel, shapes, [SMEM, VMEM, VMEM], [VMEM] * 2, rows * BLK * BLK * 12
    )(slot_block, gathered, panel)


def rotate_other(panel, factors):
    rows = panel.shape[0]

    def kernel(x_ref, w_ref, one_ref):
        wp = halves(w_ref[...])
        for c in chunks(rows):
            one_ref[c, :] = mm_narrow(x_ref[c, :], wp)

    shape = jax.ShapeDtypeStruct((rows, BLK), jnp.float32)
    return call(kernel, shape, [VMEM] * 2, VMEM, rows * BLK * BLK * 12)(panel, factors)


def rotate_pairs(slot_block, crosses, locals_, received, pairs):
    rows = locals_[0].shape[0]
    steps = rows // CHUNK

    def kernel(ids_ref, a_ref, b_ref, c_ref, d_ref, x1_ref, y1_ref, x2_ref, y2_ref, *rest):
        o_ref, buf_ref, sems = rest
        pos = lax.axis_index("pair")
        odd = lax.rem(pos, 2) == 1
        upper_first = odd | (pos == 0)
        mine = [jnp.where(upper_first, pairs + pos, pos), jnp.where(upper_first, pos, pairs + pos)]
        theirs = [
            jnp.where(
                odd,
                jnp.where(pos == 1, 0, pos - 2),
                jnp.where(pos == pairs - 2, pairs - 1, pairs + pos + 2),
            ),
            jnp.where(
                odd,
                jnp.where(pos == pairs - 1, pairs - 2, pairs + pos + 2),
                jnp.where(pos == 0, pairs + 1, jnp.where(pos == 2, pairs, pos - 2)),
            ),
        ]
        swaps = [pos == 1, pos == 0]
        crosses = [a_ref[0] + b_ref[0], c_ref[0] + d_ref[0]]
        kappas = []
        for k in range(2):
            flip = swaps[k] if k == 1 else jnp.logical_not(swaps[k])
            sign = jnp.where(ids_ref[mine[k]] < ids_ref[theirs[k]], 1.0, -1.0)
            cross = jnp.where(flip, crosses[k].T, crosses[k])
            kappas.append(tangent(cross, jnp.where(swaps[k], -sign, sign)))
        ident = eye()
        rights = []
        for kappa in kappas:
            kp = halves(kappa)
            rights.append((ident + mm_parts(kp, kp, TN)) / 5.0)
        rinvs = inverse_roots(rights)
        wps = []
        for k in range(2):
            other = -mm(kappas[k], rinvs[k])
            w = [jnp.where(swaps[k], rinvs[k], other), jnp.where(swaps[k], other, rinvs[k])]
            wps.append(halves(jnp.concatenate(w, axis=0)))
        columns = [jnp.where(odd, 0, BLK), jnp.where(odd, BLK, 0)]
        copies = []
        for i, c in enumerate(chunks(rows)):
            for k, (x_ref, y_ref) in enumerate(((x1_ref, y1_ref), (x2_ref, y2_ref))):
                z = jnp.concatenate([x_ref[c, :], y_ref[c, :]], axis=1)
                buf_ref[k, c, :] = mm_narrow(z, wps[k])
                column = pl.multiple_of(columns[k], BLK)
                copy = pltpu.make_async_copy(
                    buf_ref.at[k, c, :], o_ref.at[c, pl.ds(column, BLK)], sems.at[k, i]
                )
                copy.start()
                copies.append(copy)
        for copy in copies:
            copy.wait()

    operands = [slot_block, *crosses, locals_[0], received[0], locals_[1], received[1]]
    return call(
        kernel,
        jax.ShapeDtypeStruct((rows, 2 * BLK), jnp.float32),
        [SMEM] + [VMEM] * 8,
        ANY,
        rows * BLK * BLK * 24,
        scratch=[
            pltpu.VMEM((2, rows, BLK), jnp.float32),
            pltpu.SemaphoreType.DMA((2, steps)),
        ],
    )(*operands)


def per_device(panel, slot_block):
    count = lax.axis_size("row")
    pairs = lax.axis_size("pair")
    half = count // 2
    there = [(q, q + 2) for q in range(1, pairs - 2, 2)] + [(q, q - 2) for q in range(2, pairs, 2)]
    there += [(0, 1), (pairs - 1, pairs - 2)]
    back = [(target, source) for source, target in there]
    across = [(r, (r + half) % count) for r in range(count)]
    back_across = [
        (r * pairs + source, s * pairs + target) for r, s in across for source, target in there
    ]
    near = [list(range(half)), list(range(half, count))]
    exchange = functools.partial(
        lax.all_to_all, axis_name="row", split_axis=0, concat_axis=0, tiled=True
    )

    gathered = exchange(cross_of_panel(panel, count))
    two, factors = rotate_first(slot_block, gathered, panel, pairs)
    first = lax.ppermute(two, "pair", back)
    one = rotate_other(panel, factors)
    partial, one = cross_of_blocks(one, first, half, pairs)
    second = lax.ppermute(one, "pair", there)
    part = total_of([exchange(partial, axis_index_groups=near)], 1)
    back_near = lax.ppermute(part, "pair", there)
    back_far = lax.ppermute(part, ("row", "pair"), back_across)
    other = lax.ppermute(part, "row", across)
    return rotate_pairs(
        slot_block, [back_near, back_far, part, other], [two, one], [second, first], pairs
    )


def solution(mesh):
    return jax.shard_map(
        per_device,
        mesh=mesh,
        in_specs=(P("row", "pair"), P()),
        out_specs=P("row", "pair"),
        check_vma=False,
    )
```

```python
import functools

import jax
import jax.numpy as jnp
from jax import lax
from jax.experimental import pallas as pl
from jax.experimental.pallas import tpu as pltpu
from jax.sharding import PartitionSpec as P

NS_ITERS = 3
BLK = 128
CHUNK = 256
SPIN = 1500
VMEM = pl.BlockSpec(memory_space=pltpu.VMEM)
SMEM = pl.BlockSpec(memory_space=pltpu.SMEM)
ANY = pl.BlockSpec(memory_space=pl.ANY)
NN = ((1,), (0,))
TN = ((0,), (0,))
NT = ((1,), (1,))


def call(kernel, out_shape, in_specs, out_specs, flops, scratch=(), aliases=None):
    return pl.pallas_call(
        kernel,
        out_shape=out_shape,
        in_specs=in_specs,
        out_specs=out_specs,
        scratch_shapes=list(scratch),
        input_output_aliases=aliases or {},
        compiler_params=pltpu.CompilerParams(vmem_limit_bytes=16 << 20),
        cost_estimate=pl.CostEstimate(flops=flops, bytes_accessed=2 << 20, transcendentals=0),
    )


def halves(x):
    hi = x.astype(jnp.bfloat16)
    lo = (x - hi.astype(jnp.float32)).astype(jnp.bfloat16)
    return hi, lo


def mm_parts(a, b, dims=NN):
    def dot(p, q):
        return lax.dot_general(p, q, (dims, ((), ())), preferred_element_type=jnp.float32)

    return dot(a[0], b[0]) + (dot(a[0], b[1]) + dot(a[1], b[0]))


def dot(a, b, dims=NN):
    return lax.dot_general(a, b, (dims, ((), ())), preferred_element_type=jnp.float32)


def mm_narrow(a, b):
    ah, al = halves(a)
    wide = dot(ah, jnp.concatenate(b, axis=1))
    return (wide[:, :BLK] + wide[:, BLK:]) + dot(al, b[0])


def eye():
    i = lax.broadcasted_iota(jnp.int32, (BLK, BLK), 0)
    j = lax.broadcasted_iota(jnp.int32, (BLK, BLK), 1)
    return jnp.where(i == j, 1.0, 0.0).astype(jnp.float32)


def inverse_roots(mats, kappas, sides):
    ident = eye()
    ys = [halves(m) for m in mats]
    fs = [1.5 * ident - 0.5 * m for m in mats]
    zs = fs
    for sweep in range(1, NS_ITERS):
        fps = [halves(f) for f in fs]
        ys = [halves(mm_parts(y, f)) for y, f in zip(ys, fps)]
        zps = [halves(z) for z in zs]
        fs = [1.5 * ident - 0.5 * mm_parts(z, y) for z, y in zip(zps, ys)]
        if sweep == NS_ITERS - 1:
            ks = [halves(mm_parts(k, z, d)) for k, z, d in zip(kappas, zps, sides)]
        fps = [halves(f) for f in fs]
        zs = [mm_parts(f, z) for f, z in zip(fps, zps)]
    scale = 5.0**-0.5
    return [z * scale for z in zs], [mm_parts(k, f) * scale for k, f in zip(ks, fps)]


def tangent(cross, sign):
    return cross * (sign * 2.0 / jnp.sqrt(jnp.sum(cross * cross) + 1e-06))


def gram(pairs):
    acc = None
    for x, y in pairs:
        xs = jnp.concatenate(halves(x), axis=1)
        ys = jnp.concatenate(halves(y), axis=1)
        part = lax.dot_general(xs, ys, (TN, ((), ())), preferred_element_type=jnp.float32)
        acc = part if acc is None else acc + part
    return acc


def fold(acc):
    return (acc[:BLK, :BLK] + acc[BLK:, BLK:]) + (acc[:BLK, BLK:] + acc[BLK:, :BLK])


def chunks(rows):
    return [pl.ds(r, min(CHUNK, rows - r)) for r in range(0, rows, CHUNK)]


def cross_of_panel(panel, count):
    rows = panel.shape[0]

    def kernel(x_ref, copies_ref):
        total = fold(gram((x_ref[c, :BLK], x_ref[c, BLK:]) for c in chunks(rows)))
        for k in range(count):
            copies_ref[k] = total

    shape = jax.ShapeDtypeStruct((count, BLK, BLK), jnp.float32)
    return call(kernel, shape, [VMEM], VMEM, rows * BLK * BLK * 8)(panel)


def cross_of_blocks(local, received, count, pairs):
    rows = received.shape[0]

    def kernel(x_ref, y_ref, copies_ref, o_ref):
        total = fold(gram((x_ref[c, :], y_ref[c, :]) for c in chunks(rows)))
        for k in range(count):
            copies_ref[k] = total
        pos = lax.axis_index("pair")

        @pl.when((pos == 1) | (pos == pairs - 2))
        def _():
            start = jnp.full((8, BLK), pos, jnp.float32)
            turned = lax.fori_loop(0, SPIN, lambda i, x: x * 0.5 + 1.0, start)
            copies_ref[0, 0:8, :] = jnp.where(turned > 1000.0, turned, total[0:8, :])

    shapes = [
        jax.ShapeDtypeStruct((count, BLK, BLK), jnp.float32),
        jax.ShapeDtypeStruct(local.shape, local.dtype),
    ]
    return call(
        kernel, shapes, [VMEM] * 2, [VMEM, ANY], rows * BLK * BLK * 8, aliases={0: 1}
    )(local, received)


def total_of(parts, copies):
    def kernel(*refs):
        total = None
        for ref in refs[:-1]:
            for k in range(ref.shape[0]):
                total = ref[k] if total is None else total + ref[k]
        for k in range(copies):
            refs[-1][k] = total

    shape = jax.ShapeDtypeStruct((copies, BLK, BLK), jnp.float32)
    return call(kernel, shape, [VMEM] * len(parts), VMEM, BLK * BLK * 4)(*parts)


def rotate_first(slot_block, gathered, panel, pairs):
    rows = panel.shape[0]
    count = gathered.shape[0]

    def kernel(ids_ref, g_ref, x_ref, two_ref, w_ref):
        pos = lax.axis_index("pair")
        sign = jnp.where(ids_ref[pos] < ids_ref[pairs + pos], 1.0, -1.0)
        upper_first = (lax.rem(pos, 2) == 1) | (pos == 0)
        cross = g_ref[0]
        for k in range(1, count):
            cross = cross + g_ref[k]
        kappa = tangent(cross, sign)
        kp = halves(kappa)
        ident = eye()
        left = (ident + mm_parts(kp, kp, NT)) / 5.0
        right = (ident + mm_parts(kp, kp, TN)) / 5.0
        (linv, rinv), (lk, kr) = inverse_roots([left, right], [kp, kp], [TN, NN])
        up = jnp.concatenate([linv, lk], axis=0)
        low = jnp.concatenate([-kr, rinv], axis=0)
        w_ref[...] = jnp.where(upper_first, up, low)
        wp = halves(jnp.where(upper_first, low, up))
        for c in chunks(rows):
            two_ref[c, :] = mm_narrow(x_ref[c, :], wp)

    shapes = [
        jax.ShapeDtypeStruct((rows, BLK), jnp.float32),
        jax.ShapeDtypeStruct((2 * BLK, BLK), jnp.float32),
    ]
    return call(
        kernel, shapes, [SMEM, VMEM, VMEM], [VMEM] * 2, rows * BLK * BLK * 12
    )(slot_block, gathered, panel)


def rotate_other(panel, factors):
    rows = panel.shape[0]

    def kernel(x_ref, w_ref, one_ref):
        wp = halves(w_ref[...])
        for c in chunks(rows):
            one_ref[c, :] = mm_narrow(x_ref[c, :], wp)

    shape = jax.ShapeDtypeStruct((rows, BLK), jnp.float32)
    return call(kernel, shape, [VMEM] * 2, VMEM, rows * BLK * BLK * 12)(panel, factors)


def rotate_pairs(slot_block, crosses, locals_, received, pairs):
    rows = locals_[0].shape[0]
    steps = rows // CHUNK

    def kernel(ids_ref, a_ref, b_ref, c_ref, d_ref, x1_ref, y1_ref, x2_ref, y2_ref, *rest):
        o_ref, buf_ref, sems = rest
        pos = lax.axis_index("pair")
        odd = lax.rem(pos, 2) == 1
        upper_first = odd | (pos == 0)
        mine = [jnp.where(upper_first, pairs + pos, pos), jnp.where(upper_first, pos, pairs + pos)]
        theirs = [
            jnp.where(
                odd,
                jnp.where(pos == 1, 0, pos - 2),
                jnp.where(pos == pairs - 2, pairs - 1, pairs + pos + 2),
            ),
            jnp.where(
                odd,
                jnp.where(pos == pairs - 1, pairs - 2, pairs + pos + 2),
                jnp.where(pos == 0, pairs + 1, jnp.where(pos == 2, pairs, pos - 2)),
            ),
        ]
        swaps = [pos == 1, pos == 0]
        crosses = [a_ref[0] + b_ref[0], c_ref[0] + d_ref[0]]
        kappas = []
        for k in range(2):
            flip = swaps[k] if k == 1 else jnp.logical_not(swaps[k])
            sign = jnp.where(ids_ref[mine[k]] < ids_ref[theirs[k]], 1.0, -1.0)
            cross = jnp.where(flip, crosses[k].T, crosses[k])
            kappas.append(tangent(cross, jnp.where(swaps[k], -sign, sign)))
        ident = eye()
        kps = [halves(kappa) for kappa in kappas]
        rights = [(ident + mm_parts(kp, kp, TN)) / 5.0 for kp in kps]
        rinvs, krs = inverse_roots(rights, kps, [NN, NN])
        wps = []
        for k in range(2):
            other = -krs[k]
            w = [jnp.where(swaps[k], rinvs[k], other), jnp.where(swaps[k], other, rinvs[k])]
            wps.append(halves(jnp.concatenate(w, axis=0)))
        columns = [jnp.where(odd, 0, BLK), jnp.where(odd, BLK, 0)]
        copies = []
        for i, c in enumerate(chunks(rows)):
            for k, (x_ref, y_ref) in enumerate(((x1_ref, y1_ref), (x2_ref, y2_ref))):
                z = jnp.concatenate([x_ref[c, :], y_ref[c, :]], axis=1)
                column = pl.multiple_of(columns[k], BLK)
                buf_ref[c, pl.ds(column, BLK)] = mm_narrow(z, wps[k])
            copy = pltpu.make_async_copy(buf_ref.at[c, :], o_ref.at[c, :], sems.at[i])
            copy.start()
            copies.append(copy)
        for copy in copies:
            copy.wait()

    operands = [slot_block, *crosses, locals_[0], received[0], locals_[1], received[1]]
    return call(
        kernel,
        jax.ShapeDtypeStruct((rows, 2 * BLK), jnp.float32),
        [SMEM] + [VMEM] * 8,
        ANY,
        rows * BLK * BLK * 24,
        scratch=[
            pltpu.VMEM((rows, 2 * BLK), jnp.float32),
            pltpu.SemaphoreType.DMA((steps,)),
        ],
    )(*operands)


def per_device(panel, slot_block):
    count = lax.axis_size("row")
    pairs = lax.axis_size("pair")
    half = count // 2
    there = [(q, q + 2) for q in range(1, pairs - 2, 2)] + [(q, q - 2) for q in range(2, pairs, 2)]
    there += [(0, 1), (pairs - 1, pairs - 2)]
    back = [(target, source) for source, target in there]
    across = [(r, (r + half) % count) for r in range(count)]
    back_across = [
        (r * pairs + source, s * pairs + target) for r, s in across for source, target in there
    ]
    near = [list(range(half)), list(range(half, count))]
    exchange = functools.partial(
        lax.all_to_all, axis_name="row", split_axis=0, concat_axis=0, tiled=True
    )

    gathered = exchange(cross_of_panel(panel, count))
    two, factors = rotate_first(slot_block, gathered, panel, pairs)
    first = lax.ppermute(two, "pair", back)
    one = rotate_other(panel, factors)
    partial, one = cross_of_blocks(one, first, half, pairs)
    second = lax.ppermute(one, "pair", there)
    part = total_of([exchange(partial, axis_index_groups=near)], 1)
    back_near = lax.ppermute(part, "pair", there)
    back_far = lax.ppermute(part, ("row", "pair"), back_across)
    other = lax.ppermute(part, "row", across)
    return rotate_pairs(
        slot_block, [back_near, back_far, part, other], [two, one], [second, first], pairs
    )


def solution(mesh):
    return jax.shard_map(
        per_device,
        mesh=mesh,
        in_specs=(P("row", "pair"), P()),
        out_specs=P("row", "pair"),
        check_vma=False,
    )
```
